32 devices in a mesh: groups: 2 (over y), expert: 8 (over z, x), hidden: 2 (over core).
Axes of the slice: x: 2, y: 2, z: 4, core: 2. Of those that a mesh axis runs over, the one named last changes fastest.
Arguments:
- current: bfloat16 [2048, 2048], P(('groups', 'expert'), 'hidden'), parts along dimension 0, may hold values from -6 to 6
- previous: float32 [2048, 2048], P(('groups', 'expert'), 'hidden'), parts along dimension 0, may hold values from -6 to 6
- expert_ids: int32 [2048, 8], P(('groups', 'expert')), parts along dimension 0, may hold values from 0 to 15, all different within a row; in each aligned block of 128 rows (0 to 127, 128 to 255, ...) at most 72 rows name the same one
- gate_values: float32 [2048, 8], P(('groups', 'expert')), parts along dimension 0, may hold values from 0.1 to 1
- norm_gain: float32 [2048], replicated, may hold values from 0.1 to 1.9
- expert_gate: bfloat16 [16, 2048, 768], P('expert', 'hidden'), may hold values from -0.125 to 0.125
- expert_up: bfloat16 [16, 2048, 768], P('expert', 'hidden'), may hold values from -0.125 to 0.125
- expert_down: bfloat16 [16, 768, 2048], P('expert', None, 'hidden'), may hold values from -0.21875 to 0.21875
- dense_gate: bfloat16 [2048, 3072], P('expert', 'hidden'), may hold values from -0.125 to 0.125
- dense_up: bfloat16 [2048, 3072], P('expert', 'hidden'), may hold values from -0.125 to 0.125
- dense_down: bfloat16 [3072, 2048], P('hidden', 'expert'), may hold values from -0.109375 to 0.109375
Outputs:
- layer_out: bfloat16 [2048, 2048], P(('groups', 'expert'), 'hidden'), parts along dimension 0
The draws below stay inside these ranges and needn't reach their ends.
There are 2 independent parts, one for each index of `groups`. The reference program is written for one: setup_inputs(seed, part) draws one part's arguments, and reference() takes and returns one part's arrays. A program takes and returns all parts, laid end to end along the dimension named above; an argument that names none is the same for every part. Nothing has to cross between parts.
Inputs may be any that keep to these rules, and one draw needn't show every extreme that they name: `expert_ids`: each row names 8 different experts. Within the rows of one index of the expert axis (aligned blocks of 128 rows) no expert is named by more than 72 rows, and in every draw some expert is named by exactly 72 rows of some block.
All inputs are finite; a program needn't handle non-finite values.
Results may differ from the reference program's by a relative error of at most 0.02.
Values may be sent and summed in bfloat16 or wider, within the bound.
No kernel may reach another device: no remote copies, remote signals or barrier semaphores. Data moves between devices by JAX's collectives and lax.ppermute only.
A program may use at most 64 MiB of HBM per device.

```python
import math
import jax
import jax.numpy as jnp
import numpy as np
from jax import lax

D = 2048
F = 768
FFD = 3072
TOP_K = 8
TOK_DEV = 128
EXPERTS = 16
TOKENS = 1024
CAP = 72
N_EXPERT = 8
N_HIDDEN = 2


def shard_levels(own_key, shape, pieces, low, largest):
    factor_of = 1.0
    for dim, shards_of in pieces:
        steps = jax.random.uniform(jax.random.fold_in(jax.random.fold_in(own_key, 6), dim), (shards_of,), jnp.float32, low / len(pieces), largest / len(pieces))
        factor_of = factor_of * jnp.repeat(jnp.exp(steps), shape[dim] // shards_of).reshape((-1,) + (1,) * (len(shape) - 1 - dim))
    return factor_of


def shared_out(stream_key, own, number, rows, number_of, top, limit, skew):
    sequence = jax.random.permutation(stream_key, number_of)
    heavy_load, common = load_shares(number_of, rows * top, limit, skew, True), load_shares(number_of, rows * top, limit, skew, False)
    places = jnp.arange(number_of)

    def named(tallies, rotation):
        used = int((tallies > 0).sum())
        fixed = max(1, used // 4)
        shifted = fixed + (places - fixed + rotation * (used - fixed)) % max(1, number_of - fixed)
        return jnp.zeros((number_of,), jnp.int32).at[sequence[jnp.where(places < fixed, places, shifted)]].set(jnp.asarray(tallies, jnp.int32))

    tallies = jnp.where(number % 4 == 0, named(heavy_load, number // 4), named(common, number - number // 4 - 1))
    mixed = jax.random.permutation(jax.random.fold_in(own, 3), number_of)
    donor, receiver = mixed[0:number_of // 2 * 2:2], mixed[1:number_of // 2 * 2:2]
    room = jnp.minimum(tallies[donor] - 1, limit - tallies[receiver]) // 2
    room = jnp.where((donor == sequence[0]) | (receiver == sequence[0]) | (tallies[receiver] == 0), 0, jnp.maximum(room, 0))
    shifted = jax.random.randint(jax.random.fold_in(own, 4), (number_of // 2,), 0, 1 << 20) % (room + 1)
    tallies = tallies.at[donor].add(-shifted).at[receiver].add(shifted)
    labels = jnp.searchsorted(jnp.cumsum(tallies), jnp.arange(rows * top), side="right").astype(jnp.int32)
    listing = labels.reshape(top, rows).T
    listing = listing[jax.random.permutation(jax.random.fold_in(own, 1), rows)]
    rotation = jax.random.randint(jax.random.fold_in(own, 2), (rows, 1), 0, top)
    return jnp.take_along_axis(listing, (jnp.arange(top)[None, :] + rotation) % top, axis=1)


def load_shares(count, total, most, lean, full):
    loads = [(1 << 20) // math.isqrt(grade ** lean) + 1 for grade in range(1, count + 1)]
    largest = most if full else min(most, max(-(-total // count), total * loads[0] // sum(loads)))
    least = 1 if total - largest >= count - 1 else 0
    counts, spare = [largest] + [least] * (count - 1), total - largest - least * (count - 1)
    while spare > 0:
        movable = [i for i in range(1, count) if counts[i] < largest] or [i for i in range(1, count) if counts[i] < most]
        mass, budget = sum([loads[i] for i in movable]), spare
        for i in movable:
            more = min(most - counts[i], max(1, budget * loads[i] // mass), spare)
            counts[i] = counts[i] + more
            spare = spare - more
    return np.array(counts)


def noise(own_key, shape, deviation, limit, split=(), held_as=jnp.bfloat16):
    values = deviation * jax.random.normal(own_key, shape, jnp.float32)
    if split:
        values = values * shard_levels(own_key, shape, split, -0.22, 0.18)
    return jnp.clip(values, -limit, limit).astype(held_as)


def setup_inputs(seed: int = 0, part: int = 0) -> dict:
    seeds = jax.random.split(jax.random.key(seed), 12)
    part_splits = jax.random.split(jax.random.fold_in(seeds[11], part), 12)
    current = noise(part_splits[0], (TOKENS, D), 1.0, 6.0, ((0, 8), (1, 2)))
    previous = noise(part_splits[1], (TOKENS, D), 1.0, 6.0, ((0, 8), (1, 2)), jnp.float32)
    expert_ids_keys = jax.random.split(jax.random.fold_in(part_splits[2], 1), TOKENS // TOK_DEV)
    expert_ids_turns = jax.random.permutation(jax.random.fold_in(part_splits[2], 3), TOKENS // TOK_DEV)
    expert_ids = jax.vmap(lambda own, number: shared_out(jax.random.fold_in(part_splits[2], 2), own, number, TOK_DEV, EXPERTS, TOP_K, CAP, 2))(expert_ids_keys, expert_ids_turns).reshape((TOKENS, TOP_K))
    gate_values = jnp.clip(0.1 + 0.9 * jax.random.uniform(part_splits[3], (TOKENS, TOP_K), jnp.float32) ** shard_levels(part_splits[3], (TOKENS, TOP_K), ((0, 8),), -0.2, 0.2), 0.1, 1.0)
    norm_gain = jnp.clip(1.0 + 0.18 * jax.random.normal(seeds[4], (D,), jnp.float32), 0.1, 1.9)
    expert_gate = noise(seeds[5], (EXPERTS, D, F), D ** -0.5, 0.125, ((0, 8), (1, 2)))
    expert_up = noise(seeds[6], (EXPERTS, D, F), D ** -0.5, 0.125, ((0, 8), (1, 2)))
    expert_down = noise(seeds[7], (EXPERTS, F, D), F ** -0.5, 0.21875, ((0, 8), (2, 2)))
    dense_gate = noise(seeds[8], (D, FFD), D ** -0.5, 0.125, ((0, 8), (1, 2)))
    dense_up = noise(seeds[9], (D, FFD), D ** -0.5, 0.125, ((0, 8), (1, 2)))
    dense_down = noise(seeds[10], (FFD, D), FFD ** -0.5, 0.109375, ((0, 2), (1, 8)))
    return {"current": current, "previous": previous, "expert_ids": expert_ids, "gate_values": gate_values, "norm_gain": norm_gain, "expert_gate": expert_gate, "expert_up": expert_up, "expert_down": expert_down, "dense_gate": dense_gate, "dense_up": dense_up, "dense_down": dense_down}


def block_positions(block_ids):
    flat_ids = block_ids.reshape(-1)
    one_hot = (flat_ids[:, None] == jnp.arange(EXPERTS, dtype=jnp.int32)[None, :]).astype(jnp.int32)
    before = jnp.cumsum(one_hot, axis=0) - one_hot
    return lax.optimization_barrier(jnp.sum(before * one_hot, axis=1)).astype(jnp.int32)

def reference(current, previous, expert_ids, gate_values, norm_gain, expert_gate, expert_up, expert_down, dense_gate, dense_up, dense_down):
    slice_width = D // N_HIDDEN
    per_expert = N_EXPERT * CAP
    routed = previous.astype(jnp.bfloat16)
    routed_pad = jnp.concatenate([routed, jnp.zeros((1, D), jnp.bfloat16)], axis=0)
    position = jax.vmap(block_positions)(expert_ids.reshape(N_EXPERT, TOK_DEV, TOP_K)).reshape(-1)
    flat_ids = expert_ids.reshape(-1).astype(jnp.int32)
    token_of = (jnp.arange(TOKENS * TOP_K, dtype=jnp.int32) // TOP_K).astype(jnp.int32)
    source = (token_of // TOK_DEV).astype(jnp.int32)
    place = (flat_ids * per_expert + source * CAP + position).astype(jnp.int32)
    table = jnp.full((EXPERTS * per_expert,), TOKENS, jnp.int32).at[place].set(token_of)
    table = table.reshape(EXPERTS, per_expert)

    def one_expert(inputs):
        rows_index, w_gate, w_up, w_down = inputs
        rows = routed_pad[rows_index].astype(jnp.float32).reshape(per_expert, N_HIDDEN, slice_width)
        gate_part = jnp.einsum('rhd,hdf->hrf', rows, w_gate.astype(jnp.float32).reshape(N_HIDDEN, slice_width, F))
        up_part = jnp.einsum('rhd,hdf->hrf', rows, w_up.astype(jnp.float32).reshape(N_HIDDEN, slice_width, F))
        gate_low = lax.optimization_barrier(gate_part.astype(jnp.bfloat16))
        up_low = lax.optimization_barrier(up_part.astype(jnp.bfloat16))
        gate_sum = lax.optimization_barrier(jnp.sum(gate_low.astype(jnp.float32), axis=0))
        up_sum = lax.optimization_barrier(jnp.sum(up_low.astype(jnp.float32), axis=0))
        act = (jax.nn.silu(gate_sum) * up_sum).astype(jnp.bfloat16)
        return jnp.dot(act, w_down, preferred_element_type=jnp.float32).astype(jnp.bfloat16)
    outputs = lax.map(one_expert, (table, expert_gate, expert_up, expert_down)).reshape(EXPERTS * per_expert, D)
    place_grid = place.reshape(TOKENS, TOP_K)
    routed_sum = jnp.zeros((TOKENS, D), jnp.float32)
    for choice_index in range(TOP_K):
        picked = outputs[place_grid[:, choice_index]].astype(jnp.float32)
        routed_sum = routed_sum + gate_values[:, choice_index][:, None] * picked
    wide = current.astype(jnp.float32)
    mean_square = lax.optimization_barrier(jnp.mean(wide * wide, axis=1, keepdims=True))
    normed = (wide * norm_gain[None, :] / jnp.sqrt(mean_square + 1e-06)).astype(jnp.bfloat16)
    gate_dense = jnp.dot(normed, dense_gate, preferred_element_type=jnp.float32)
    up_dense = jnp.dot(normed, dense_up, preferred_element_type=jnp.float32)
    dense_act = (jax.nn.silu(gate_dense) * up_dense).astype(jnp.bfloat16)
    share = FFD // N_HIDDEN
    dense_sum = jnp.zeros((TOKENS, D), jnp.float32)
    for part_index in range(N_HIDDEN):
        term = jnp.dot(dense_act[:, part_index * share:(part_index + 1) * share], dense_down[part_index * share:(part_index + 1) * share], preferred_element_type=jnp.float32)
        term_low = lax.optimization_barrier(term.astype(jnp.bfloat16))
        dense_sum = dense_sum + term_low.astype(jnp.float32)
    return (dense_sum + routed_sum).astype(jnp.bfloat16)
```

```python
import functools

import jax
import jax.numpy as jnp
from jax import lax
from jax.experimental import pallas as pl
from jax.experimental.pallas import tpu as pltpu
from jax.sharding import PartitionSpec as P

TOP_K = 8
LANES = 128


def slot_places(expert_ids, experts_all, owned, owners, capacity):
    flat_ids = expert_ids.reshape(-1)
    one_hot = (flat_ids[:, None] == jnp.arange(experts_all, dtype=jnp.int32)[None, :]).astype(
        jnp.int32
    )
    before = jnp.cumsum(one_hot, axis=0) - one_hot
    position = jnp.sum(before * one_hot, axis=1)
    return flat_ids % owned * (owners * capacity) + flat_ids // owned * capacity + position


def routed_branch(previous, expert_ids, gate_values, expert_gate, expert_up, expert_down):
    tokens_here, slice_width = previous.shape
    owned = expert_gate.shape[0]
    owners = lax.axis_size("expert")
    experts_all = owned * owners
    capacity = min(tokens_here, tokens_here * TOP_K * 9 // (8 * experts_all))
    places = slot_places(expert_ids, experts_all, owned, owners, capacity)
    token_of = jnp.arange(tokens_here * TOP_K, dtype=jnp.int32) // TOP_K
    table = jnp.full((experts_all * capacity,), tokens_here, jnp.int32).at[places].set(token_of)
    routed = previous.astype(jnp.bfloat16)
    routed_pad = jnp.concatenate([routed, jnp.zeros((1, slice_width), jnp.bfloat16)], axis=0)
    outgoing = routed_pad[table].reshape(owned, owners, capacity, slice_width)
    arrived = lax.all_to_all(outgoing, "expert", split_axis=1, concat_axis=1, tiled=True)
    arrived = arrived.reshape(owned, owners * capacity, slice_width)
    gate_part = jnp.einsum("erd,edf->erf", arrived, expert_gate, preferred_element_type=jnp.float32)
    up_part = jnp.einsum("erd,edf->erf", arrived, expert_up, preferred_element_type=jnp.float32)
    gate_sum, up_sum = (
        lax.psum(gate_part.astype(jnp.bfloat16), "hidden").astype(jnp.float32),
        lax.psum(up_part.astype(jnp.bfloat16), "hidden").astype(jnp.float32),
    )
    activated = (jax.nn.silu(gate_sum) * up_sum).astype(jnp.bfloat16)
    produced = jnp.einsum(
        "erf,efd->erd", activated, expert_down, preferred_element_type=jnp.float32
    ).astype(jnp.bfloat16)
    produced = produced.reshape(owned, owners, capacity, slice_width)
    returned = lax.all_to_all(produced, "expert", split_axis=1, concat_axis=1, tiled=True)
    returned = returned.reshape(experts_all * capacity, slice_width)
    picked = returned[places].reshape(tokens_here, TOP_K, slice_width).astype(jnp.float32)
    return jnp.einsum("tk,tkd->td", gate_values, picked)


def dense_branch(current, norm_gain, dense_gate, dense_up, dense_down):
    whole = lax.all_gather(current, "hidden", axis=1, tiled=True)
    wide = whole.astype(jnp.float32)
    mean_square = jnp.mean(wide * wide, axis=1, keepdims=True)
    normed = (wide * norm_gain[None, :] / jnp.sqrt(mean_square + 1e-06)).astype(jnp.bfloat16)
    full_gate, full_up = (
        lax.all_gather(dense_gate, "expert", axis=0, tiled=True),
        lax.all_gather(dense_up, "expert", axis=0, tiled=True),
    )
    gate_dense = jnp.dot(normed, full_gate, preferred_element_type=jnp.float32)
    up_dense = jnp.dot(normed, full_up, preferred_element_type=jnp.float32)
    dense_act = (jax.nn.silu(gate_dense) * up_dense).astype(jnp.bfloat16)
    terms = jnp.dot(
        dense_act,
        lax.all_gather(dense_down, "expert", axis=1, tiled=True),
        preferred_element_type=jnp.float32,
    )
    return lax.psum_scatter(
        terms.astype(jnp.bfloat16), "hidden", scatter_dimension=1, tiled=True
    ).astype(jnp.float32)


def local_general(
    current,
    previous,
    expert_ids,
    gate_values,
    norm_gain,
    expert_gate,
    expert_up,
    expert_down,
    dense_gate,
    dense_up,
    dense_down,
):
    routed_sum = routed_branch(
        previous, expert_ids, gate_values, expert_gate, expert_up, expert_down
    )
    dense_sum = dense_branch(current, norm_gain, dense_gate, dense_up, dense_down)
    return (dense_sum + routed_sum).astype(jnp.bfloat16)


def dot(a, b):
    return jnp.dot(a, b, preferred_element_type=jnp.float32)


def from_far(value, step):
    count = lax.axis_size("expert")
    return lax.ppermute(value, "expert", [(i, (i - 2 * step) % count) for i in range(count)])


def to_far(value, step):
    count = lax.axis_size("expert")
    return lax.ppermute(value, "expert", [(i, (i + 2 * step) % count) for i in range(count)])


def swap_near(value):
    count = lax.axis_size("expert")
    return lax.ppermute(value, "expert", [(i, i ^ 1) for i in range(count)])


def swap_hidden(value):
    return lax.ppermute(value, "hidden", [(0, 1), (1, 0)])


def swap_groups(value):
    return lax.ppermute(value, "groups", [(0, 1), (1, 0)])


def far_order(half):
    return sorted(range(1, half), key=lambda k: -min(k, half - k))


SMEM = pl.BlockSpec(memory_space=pltpu.SMEM)
VMEM = pl.BlockSpec(memory_space=pltpu.VMEM)


def prepare(previous, current, expert_ids, gate_values, experts_all):
    tokens, width = previous.shape

    def kernel(prev_ref, cur_ref, ids_ref, gates_ref, out_ref):
        out_ref[:, :width] = prev_ref[...].astype(jnp.bfloat16)
        cur = cur_ref[...]
        out_ref[:, width : 2 * width] = cur
        wide = cur.astype(jnp.float32)
        square = jnp.sum(wide * wide, axis=1, keepdims=True)
        lane = lax.broadcasted_iota(jnp.int32, (tokens, LANES), 1)
        expert = jnp.where(lane < experts_all, lane, lane - experts_all)
        values = jnp.zeros((tokens, LANES), jnp.float32)
        for k in range(TOP_K):
            hit = expert == ids_ref[:, k : k + 1]
            values = values + jnp.where(hit, gates_ref[:, k : k + 1], 0.0)
        values = jnp.where(lane < 2 * experts_all, values, square)
        high = values.astype(jnp.bfloat16).astype(jnp.float32)
        use_low = (lane >= experts_all) & (lane != 2 * experts_all)
        out_ref[:, 2 * width :] = jnp.where(use_low, values - high, high).astype(jnp.bfloat16)

    return pl.pallas_call(
        kernel,
        out_shape=jax.ShapeDtypeStruct((tokens, 2 * width + LANES), jnp.bfloat16),
        in_specs=[VMEM] * 4,
        out_specs=VMEM,
        name="prepare",
    )(previous, current, expert_ids, gate_values)


def pack_weights(place, gain, dense_gate, dense_up, dense_down, count):
    rows, columns = dense_gate.shape
    share = columns // count
    main, rest = share // LANES * LANES, share % LANES
    half = rows // 2
    low = dense_down.shape[1] // 4
    chips = count // 2

    def kernel(place_ref, gain_ref, gate_ref, up_ref, down_ref, *outs):
        e, g = place_ref[0], place_ref[2]
        line = gain_ref[pl.ds(e * (rows // LANES) + g, 1), :]
        row = lax.broadcasted_iota(jnp.int32, (LANES, LANES), 0)
        lane = lax.broadcasted_iota(jnp.int32, (LANES, LANES), 1)
        scale = jnp.sum(jnp.where(row == lane, line, 0.0), axis=1, keepdims=True)
        rows_here = pl.ds(pl.multiple_of(g * half, LANES), half)
        columns_here = pl.ds(pl.multiple_of(g * 2 * low, LANES), 2 * low)

        def scaled(ref, start):
            block = ref[rows_here, pl.ds(pl.multiple_of(start, LANES), LANES)]
            return block.astype(jnp.float32) * scale

        for index, out_ref in enumerate(outs):
            a, k = index // chips, index % chips
            owner = ((e + 2 * k) % count) ^ a
            out_ref[:half, :main] = scaled(gate_ref, owner * main).astype(jnp.bfloat16)
            out_ref[:half, main : 2 * main] = scaled(up_ref, owner * main).astype(jnp.bfloat16)
            spot = count * main + owner // 2 * LANES
            tail_gate, tail_up = scaled(gate_ref, spot), scaled(up_ref, spot)
            even = jnp.concatenate([tail_gate[:, :rest], tail_up[:, :rest]], axis=1)
            odd = jnp.concatenate([tail_gate[:, rest:], tail_up[:, rest:]], axis=1)
            out_ref[:half, 2 * main :] = jnp.where(owner % 2 == 0, even, odd).astype(jnp.bfloat16)
            for i in range(main // low):
                start = pl.multiple_of(owner * main + i * low, low)
                out_ref[half:, i * LANES : (i + 1) * LANES] = down_ref[pl.ds(start, low), columns_here]
            start = pl.multiple_of(count * main + owner * rest, rest)
            out_ref[half:, main // low * LANES :] = down_ref[pl.ds(start, low), columns_here]

    block = jax.ShapeDtypeStruct((half + low, 2 * share), jnp.bfloat16)
    return pl.pallas_call(
        kernel,
        out_shape=[block] * count,
        in_specs=[SMEM] + [VMEM] * 4,
        out_specs=[VMEM] * count,
        name="pack",
    )(place, gain, dense_gate, dense_up, dense_down)


def stacked(blocks):
    def kernel(*refs):
        for i, ref in enumerate(refs[:-1]):
            refs[-1][i] = ref[...]

    return pl.pallas_call(
        kernel,
        out_shape=jax.ShapeDtypeStruct((len(blocks),) + blocks[0].shape, blocks[0].dtype),
        in_specs=[VMEM] * len(blocks),
        out_specs=VMEM,
        name="stack",
    )(*blocks)


def assemble(place, mine, other, count, width):
    part, wide = mine[0].shape[1:]
    share = wide // 2
    half = LANES
    low = part - half
    chips, span = count // 2, count // 2

    def kernel(place_ref, *refs):
        rows_ref, here_ref, there_ref = refs[-3:]
        e, h, g = place_ref[0], place_ref[1], place_ref[2]
        first, second = refs[: len(mine)], refs[len(mine) : len(mine) + len(other)]
        for stacks, group in ((first, g), (second, 1 - g)):
            index = 0
            for stack in stacks:
                for i in range(stack.shape[0]):
                    a, k = index // chips, index % chips
                    index += 1
                    source = ((e + 2 * k) % count) ^ a
                    spot = jnp.bitwise_xor(source // span, h) * span + source % span
                    start = pl.multiple_of(spot * 2 * half + group * half, half)
                    rows_ref[pl.ds(start, half), :] = stack[i, :half]
                    lane = pl.ds(pl.multiple_of(source % span * 2 * half + group * half, half), half)

                    @pl.when(source // span == h)
                    def _():
                        for j in range(share // low):
                            here_ref[j * low : (j + 1) * low, lane] = stack[i, half:, j * half : (j + 1) * half]

                    @pl.when(source // span != h)
                    def _():
                        for j in range(share // low):
                            there_ref[j * low : (j + 1) * low, lane] = stack[i, half:, j * half : (j + 1) * half]

    down = jax.ShapeDtypeStruct((share, width), jnp.bfloat16)
    return pl.pallas_call(
        kernel,
        out_shape=[jax.ShapeDtypeStruct((2 * width, wide), jnp.bfloat16), down, down],
        in_specs=[SMEM] + [VMEM] * (len(mine) + len(other)),
        out_specs=[VMEM] * 3,
        name="assemble",
    )(place, *mine, *other)


def activations(place, pieces, others, gate, up, gate_in, up_in, dense_rows, experts_all):
    tokens, width = pieces[0].shape[0], gate.shape[1]
    units = gate.shape[2]
    owned = gate.shape[0]
    share = dense_rows.shape[1] // 2
    main = share // LANES * LANES
    rest = share - main
    tile = 256
    many = len(pieces)
    rows = many * tokens
    total = -(-(units + share) // LANES) * LANES

    def kernel(place_ref, *refs):
        own, far = refs[:many], refs[many : 2 * many]
        gate_ref, up_ref, gate_in_ref, up_in_ref, dense_ref = refs[2 * many : 2 * many + 5]
        out_ref, x_ref, weight_ref = refs[2 * many + 5 :]
        step = pl.program_id(0)

        @pl.when(step == 0)
        def _():
            for i in range(many):
                here = slice(i * tokens, (i + 1) * tokens)
                for side, ref in enumerate((own[i], far[i])):
                    x_ref[here, side * width : (side + 1) * width] = ref[:, :width]
                table = own[i][:, 2 * width :].astype(jnp.float32)
                lane = lax.broadcasted_iota(jnp.int32, (tokens, LANES), 1)
                expert = place_ref[0] * owned + place_ref[1]
                hit = (lane == expert) | (lane == expert + experts_all)
                weight_ref[here, :] = jnp.sum(jnp.where(hit, table, 0.0), axis=1, keepdims=True)
                table = table + far[i][:, 2 * width :].astype(jnp.float32)
                hit = (lane == 2 * experts_all) | (lane == 2 * experts_all + 1)
                square = jnp.sum(jnp.where(hit, table, 0.0), axis=1, keepdims=True)
                scale = 1.0 / jnp.sqrt(square / (2 * width) + 1e-06)
                both = dot(own[i][:, width : 2 * width], dense_ref[:width])
                both = both + dot(far[i][:, width : 2 * width], dense_ref[width:])
                both = both * scale
                act = jax.nn.silu(both[:, :main]) * both[:, main : 2 * main]
                out_ref[here, units : units + main] = act.astype(jnp.bfloat16)
                tail = jax.nn.silu(both[:, 2 * main : 2 * main + rest]) * both[:, 2 * main + rest :]
                spare = jnp.zeros((tokens, total - units - share), jnp.float32)
                out_ref[here, units + main :] = jnp.concatenate([tail, spare], axis=1).astype(jnp.bfloat16)

        gate_sum = dot(x_ref[:, :width], gate_ref[0]) + dot(x_ref[:, width:], gate_in_ref[...])
        up_sum = dot(x_ref[:, :width], up_ref[0]) + dot(x_ref[:, width:], up_in_ref[...])
        act = jax.nn.silu(gate_sum) * up_sum * weight_ref[...]
        out_ref[:, pl.ds(pl.multiple_of(step * tile, tile), tile)] = act.astype(jnp.bfloat16)

    def whole(a):
        return pl.BlockSpec(a.shape, lambda j, s: (0, 0))

    own_weight = pl.BlockSpec((1, width, tile), lambda j, s: (s[1], 0, j))
    far_weight = pl.BlockSpec((width, tile), lambda j, s: (0, j))
    return pl.pallas_call(
        kernel,
        grid_spec=pltpu.PrefetchScalarGridSpec(
            num_scalar_prefetch=1,
            grid=(units // tile,),
            in_specs=[whole(p) for p in (*pieces, *others)]
            + [own_weight, own_weight, far_weight, far_weight, whole(dense_rows)],
            out_specs=pl.BlockSpec((rows, total), lambda j, s: (0, 0)),
            scratch_shapes=[
                pltpu.VMEM((rows, 2 * width), jnp.bfloat16),
                pltpu.VMEM((rows, 1), jnp.float32),
            ],
        ),
        out_shape=jax.ShapeDtypeStruct((rows, total), jnp.bfloat16),
        cost_estimate=pl.CostEstimate(
            flops=4 * rows * width * (2 * units + share * 2),
            bytes_accessed=8 * width * units + 2 * rows * 4 * width,
            transcendentals=rows * (units + share),
        ),
        name="activations",
    )(place, *pieces, *others, gate, up, gate_in, up_in, dense_rows)


def products(place, act, act_in, down, dense_here, dense_in, tokens):
    rows = act.shape[0]
    units, width = down.shape[1], down.shape[2]
    share = dense_here.shape[0]
    tile = 512

    def kernel(place_ref, act_ref, in_ref, down_ref, down_far_ref, here_ref, far_ref, keep_ref, send_ref):
        total = dot(act_ref[:, :units], down_ref[0]) + dot(in_ref[:, :units], down_far_ref[0])
        total = total + dot(act_ref[:, units : units + share], here_ref[...])
        total = total + dot(in_ref[:, units : units + share], far_ref[...])
        keep_ref[...] = total[:tokens]
        send_ref[...] = total[tokens:].astype(jnp.bfloat16)

    whole = pl.BlockSpec(act.shape, lambda j, s: (0, 0))
    dense = pl.BlockSpec((share, tile), lambda j, s: (0, j))
    piece = pl.BlockSpec((tokens, tile), lambda j, s: (0, j))
    return pl.pallas_call(
        kernel,
        grid_spec=pltpu.PrefetchScalarGridSpec(
            num_scalar_prefetch=1,
            grid=(width // tile,),
            in_specs=[
                whole,
                whole,
                pl.BlockSpec((1, units, tile), lambda j, s: (s[1], 0, j)),
                pl.BlockSpec((1, units, tile), lambda j, s: (1 - s[1], 0, j)),
                dense,
                dense,
            ],
            out_specs=[piece, piece],
        ),
        out_shape=[
            jax.ShapeDtypeStruct((tokens, width), jnp.float32),
            jax.ShapeDtypeStruct((rows - tokens, width), jnp.bfloat16),
        ],
        cost_estimate=pl.CostEstimate(
            flops=4 * rows * width * (units + share),
            bytes_accessed=4 * width * (units + share) + 4 * rows * width,
            transcendentals=0,
        ),
        name="products",
    )(place, act, act_in, down, down, dense_here, dense_in)


def local_tiled(
    current,
    previous,
    expert_ids,
    gate_values,
    norm_gain,
    expert_gate,
    expert_up,
    expert_down,
    dense_gate,
    dense_up,
    dense_down,
):
    tokens, width = previous.shape
    owned = expert_gate.shape[0]
    count = lax.axis_size("expert")
    chips = count // 2
    experts_all = owned * count
    h = lax.axis_index("hidden")
    place = jnp.stack([lax.axis_index("expert"), h, lax.axis_index("groups")]).astype(jnp.int32)

    piece = prepare(previous, current, expert_ids, gate_values, experts_all)
    far = {0: piece}
    for k in far_order(chips):
        far[k] = from_far(piece, k)
    near = {k: swap_near(far[k]) for k in [0] + far_order(chips)}

    packed = pack_weights(place, norm_gain.reshape(-1, LANES), dense_gate, dense_up, dense_down, count)
    got = {(0, 0): packed[0]}
    for k in [0] + far_order(chips):
        for a in (0, 1):
            if k or a:
                pairs = [(i, ((i + 2 * k) % count) ^ a) for i in range(count)]
                got[a, -k % chips] = lax.ppermute(packed[a * chips + k], "expert", pairs)
    mine = [stacked([got[a, k] for k in range(chips)]) for a in (0, 1)]
    other = [swap_groups(m) for m in mine]
    dense_rows, dense_here, dense_there = assemble(place, mine, other, count, width)
    dense_in = swap_hidden(dense_there)

    gate_in = swap_hidden(lax.dynamic_index_in_dim(expert_gate, 1 - h, 0, keepdims=False))
    up_in = swap_hidden(lax.dynamic_index_in_dim(expert_up, 1 - h, 0, keepdims=False))

    result = None
    for k in far_order(chips) + [0]:
        pieces = [far[k], near[k]]
        others = [swap_hidden(p) for p in pieces]
        act = activations(
            place, pieces, others, expert_gate, expert_up, gate_in, up_in, dense_rows, experts_all
        )
        keep, send = products(place, act, swap_hidden(act), expert_down, dense_here, dense_in, tokens)
        line = keep + swap_near(send).astype(jnp.float32)
        if k:
            line = to_far(line.astype(jnp.bfloat16), k).astype(jnp.float32)
        result = line if result is None else result + line
    return result.astype(jnp.bfloat16)


def local(*args):
    current, expert_gate, dense_gate, dense_down = args[0], args[5], args[8], args[10]
    count, cores, groups = (lax.axis_size(n) for n in ("expert", "hidden", "groups"))
    share = dense_gate.shape[1] // count
    tiled = (
        cores == groups == expert_gate.shape[0] == 2
        and count % 2 == 0
        and share % LANES * 2 == LANES
        and dense_gate.shape[0] == dense_down.shape[1] == 2 * LANES
        and expert_gate.shape[2] % 256 == 0
        and current.shape[1] % 512 == 0
        and 2 * expert_gate.shape[0] * count + 2 <= LANES
    )
    return local_tiled(*args) if tiled else local_general(*args)


def solution(mesh):
    placed = (
        P(("groups", "expert"), "hidden"),
        P(("groups", "expert"), "hidden"),
        P(("groups", "expert"), None),
        P(("groups", "expert"), None),
        P(),
        P("expert", "hidden", None),
        P("expert", "hidden", None),
        P("expert", None, "hidden"),
        P("expert", "hidden"),
        P("expert", "hidden"),
        P("hidden", "expert"),
    )
    return jax.shard_map(
        local,
        mesh=mesh,
        in_specs=placed,
        out_specs=P(("groups", "expert"), "hidden"),
        check_vma=False,
    )
```

```python
import jax
import jax.numpy as jnp
from jax import lax
from jax.experimental import pallas as pl
from jax.experimental.pallas import tpu as pltpu
from jax.sharding import PartitionSpec as P

TOP_K = 8
LANES = 128


def slot_places(expert_ids, experts_all, owned, owners, capacity):
    flat_ids = expert_ids.reshape(-1)
    one_hot = (flat_ids[:, None] == jnp.arange(experts_all, dtype=jnp.int32)[None, :]).astype(
        jnp.int32
    )
    before = jnp.cumsum(one_hot, axis=0) - one_hot
    position = jnp.sum(before * one_hot, axis=1)
    return flat_ids % owned * (owners * capacity) + flat_ids // owned * capacity + position


def routed_branch(previous, expert_ids, gate_values, expert_gate, expert_up, expert_down):
    tokens_here, slice_width = previous.shape
    owned = expert_gate.shape[0]
    owners = lax.axis_size("expert")
    experts_all = owned * owners
    capacity = min(tokens_here, tokens_here * TOP_K * 9 // (8 * experts_all))
    places = slot_places(expert_ids, experts_all, owned, owners, capacity)
    token_of = jnp.arange(tokens_here * TOP_K, dtype=jnp.int32) // TOP_K
    table = jnp.full((experts_all * capacity,), tokens_here, jnp.int32).at[places].set(token_of)
    routed = previous.astype(jnp.bfloat16)
    routed_pad = jnp.concatenate([routed, jnp.zeros((1, slice_width), jnp.bfloat16)], axis=0)
    outgoing = routed_pad[table].reshape(owned, owners, capacity, slice_width)
    arrived = lax.all_to_all(outgoing, "expert", split_axis=1, concat_axis=1, tiled=True)
    arrived = arrived.reshape(owned, owners * capacity, slice_width)
    gate_part = jnp.einsum("erd,edf->erf", arrived, expert_gate, preferred_element_type=jnp.float32)
    up_part = jnp.einsum("erd,edf->erf", arrived, expert_up, preferred_element_type=jnp.float32)
    gate_sum, up_sum = (
        lax.psum(gate_part.astype(jnp.bfloat16), "hidden").astype(jnp.float32),
        lax.psum(up_part.astype(jnp.bfloat16), "hidden").astype(jnp.float32),
    )
    activated = (jax.nn.silu(gate_sum) * up_sum).astype(jnp.bfloat16)
    produced = jnp.einsum(
        "erf,efd->erd", activated, expert_down, preferred_element_type=jnp.float32
    ).astype(jnp.bfloat16)
    produced = produced.reshape(owned, owners, capacity, slice_width)
    returned = lax.all_to_all(produced, "expert", split_axis=1, concat_axis=1, tiled=True)
    returned = returned.reshape(experts_all * capacity, slice_width)
    picked = returned[places].reshape(tokens_here, TOP_K, slice_width).astype(jnp.float32)
    return jnp.einsum("tk,tkd->td", gate_values, picked)


def dense_branch(current, norm_gain, dense_gate, dense_up, dense_down):
    whole = lax.all_gather(current, "hidden", axis=1, tiled=True)
    wide = whole.astype(jnp.float32)
    mean_square = jnp.mean(wide * wide, axis=1, keepdims=True)
    normed = (wide * norm_gain[None, :] / jnp.sqrt(mean_square + 1e-06)).astype(jnp.bfloat16)
    full_gate, full_up = (
        lax.all_gather(dense_gate, "expert", axis=0, tiled=True),
        lax.all_gather(dense_up, "expert", axis=0, tiled=True),
    )
    gate_dense = jnp.dot(normed, full_gate, preferred_element_type=jnp.float32)
    up_dense = jnp.dot(normed, full_up, preferred_element_type=jnp.float32)
    dense_act = (jax.nn.silu(gate_dense) * up_dense).astype(jnp.bfloat16)
    terms = jnp.dot(
        dense_act,
        lax.all_gather(dense_down, "expert", axis=1, tiled=True),
        preferred_element_type=jnp.float32,
    )
    return lax.psum_scatter(
        terms.astype(jnp.bfloat16), "hidden", scatter_dimension=1, tiled=True
    ).astype(jnp.float32)


def local_general(
    current,
    previous,
    expert_ids,
    gate_values,
    norm_gain,
    expert_gate,
    expert_up,
    expert_down,
    dense_gate,
    dense_up,
    dense_down,
):
    routed_sum = routed_branch(
        previous, expert_ids, gate_values, expert_gate, expert_up, expert_down
    )
    dense_sum = dense_branch(current, norm_gain, dense_gate, dense_up, dense_down)
    return (dense_sum + routed_sum).astype(jnp.bfloat16)


def dot(a, b):
    return jnp.dot(a, b, preferred_element_type=jnp.float32)


def exchange(value, axis, flip):
    pairs = [(i, i ^ flip) for i in range(lax.axis_size(axis))]
    return lax.ppermute(value, axis, pairs)


def run(kernel, operands, mebibytes, **options):
    return pl.pallas_call(
        kernel, compiler_params=pltpu.CompilerParams(vmem_limit_bytes=mebibytes << 20) if mebibytes else None, **options
    )(*operands)


SMEM = pl.BlockSpec(memory_space=pltpu.SMEM)
VMEM = pl.BlockSpec(memory_space=pltpu.VMEM)


def prepare(previous, current, expert_ids, gate_values, experts_all):
    tokens, width = previous.shape

    def kernel(prev_ref, cur_ref, ids_ref, gates_ref, out_ref):
        out_ref[:, :width] = prev_ref[...].astype(jnp.bfloat16)
        cur = cur_ref[...]
        out_ref[:, width : 2 * width] = cur
        wide = cur.astype(jnp.float32)
        square = jnp.sum(wide * wide, axis=1, keepdims=True)
        lane = lax.broadcasted_iota(jnp.int32, (tokens, LANES), 1)
        expert = jnp.where(lane < experts_all, lane, lane - experts_all)
        values = jnp.zeros((tokens, LANES), jnp.float32)
        for k in range(TOP_K):
            hit = expert == ids_ref[:, k : k + 1]
            values = values + jnp.where(hit, gates_ref[:, k : k + 1], 0.0)
        values = jnp.where(lane < 2 * experts_all, values, square)
        high = values.astype(jnp.bfloat16).astype(jnp.float32)
        use_low = (lane >= experts_all) & (lane != 2 * experts_all)
        out_ref[:, 2 * width :] = jnp.where(use_low, values - high, high).astype(jnp.bfloat16)

    return run(
        kernel,
        (previous, current, expert_ids, gate_values),
        0,
        out_shape=jax.ShapeDtypeStruct((tokens, 2 * width + LANES), jnp.bfloat16),
        in_specs=[VMEM] * 4,
        out_specs=VMEM,
    )


def pack_weights(place, gain, dense_gate, dense_up, dense_down, count):
    rows, columns = dense_gate.shape
    share = columns // count
    main, rest = share // LANES * LANES, share % LANES
    half = rows // 2
    low = dense_down.shape[1] // 4

    def kernel(place_ref, gain_ref, gate_ref, up_ref, down_ref, *outs):
        e, g = place_ref[0], place_ref[2]
        line = gain_ref[pl.ds(e * (rows // LANES) + g, 1), :]
        row = lax.broadcasted_iota(jnp.int32, (LANES, LANES), 0)
        lane = lax.broadcasted_iota(jnp.int32, (LANES, LANES), 1)
        scale = jnp.sum(jnp.where(row == lane, line, 0.0), axis=1, keepdims=True)
        rows_here = pl.ds(pl.multiple_of(g * half, LANES), half)
        columns_here = pl.ds(pl.multiple_of(g * 2 * low, LANES), 2 * low)

        def scaled(ref, start):
            block = ref[rows_here, pl.ds(pl.multiple_of(start, LANES), LANES)]
            return block.astype(jnp.float32) * scale

        for index, out_ref in enumerate(outs):
            owner = jnp.bitwise_xor(e, index)
            out_ref[:half, :main] = scaled(gate_ref, owner * main).astype(jnp.bfloat16)
            out_ref[:half, main : 2 * main] = scaled(up_ref, owner * main).astype(jnp.bfloat16)
            spot = count * main + owner // 2 * LANES
            tail_gate, tail_up = scaled(gate_ref, spot), scaled(up_ref, spot)
            even = jnp.concatenate([tail_gate[:, :rest], tail_up[:, :rest]], axis=1)
            odd = jnp.concatenate([tail_gate[:, rest:], tail_up[:, rest:]], axis=1)
            out_ref[:half, 2 * main :] = jnp.where(owner % 2 == 0, even, odd).astype(jnp.bfloat16)
            for i in range(main // low):
                start = pl.multiple_of(owner * main + i * low, low)
                out_ref[half:, i * LANES : (i + 1) * LANES] = down_ref[pl.ds(start, low), columns_here]
            start = pl.multiple_of(count * main + owner * rest, rest)
            out_ref[half:, main // low * LANES :] = down_ref[pl.ds(start, low), columns_here]

    block = jax.ShapeDtypeStruct((half + low, 2 * share), jnp.bfloat16)
    return run(
        kernel,
        (place, gain, dense_gate, dense_up, dense_down),
        0,
        out_shape=[block] * count,
        in_specs=[SMEM] + [VMEM] * 4,
        out_specs=[VMEM] * count,
    )


def assemble(place, mine, other, count, width):
    part, wide = mine[0].shape
    share = wide // 2
    half = LANES
    low = part - half
    span = count // 2

    def kernel(place_ref, *refs):
        rows_ref, here_ref, there_ref = refs[-3:]
        e, h, g = place_ref[0], place_ref[1], place_ref[2]
        for blocks, group in ((refs[:count], g), (refs[count : 2 * count], 1 - g)):
            for index, block in enumerate(blocks):
                source = jnp.bitwise_xor(e, index)
                spot = jnp.bitwise_xor(source // span, h) * span + source % span
                start = pl.multiple_of(spot * 2 * half + group * half, half)
                rows_ref[pl.ds(start, half), :] = block[:half]
                lane = pl.ds(pl.multiple_of(source % span * 2 * half + group * half, half), half)
                for side, out_ref in ((h, here_ref), (1 - h, there_ref)):

                    @pl.when(source // span == side)
                    def _():
                        for j in range(share // low):
                            out_ref[j * low : (j + 1) * low, lane] = block[half:, j * half : (j + 1) * half]

    down = jax.ShapeDtypeStruct((share, width), jnp.bfloat16)
    return run(
        kernel,
        (place, *mine, *other),
        10,
        out_shape=[jax.ShapeDtypeStruct((2 * width, wide), jnp.bfloat16), down, down],
        in_specs=[SMEM] + [VMEM] * (2 * count),
        out_specs=[VMEM] * 3,
    )


def activations(place, pieces, others, gate, up, gate_in, up_in, dense_rows, experts_all):
    tokens, width = pieces[0].shape[0], gate.shape[1]
    owned, units = gate.shape[0], gate.shape[2]
    wide = dense_rows.shape[1]
    share = wide // 2
    main = share // LANES * LANES
    rest = share - main
    tile = 256
    steps = units // tile
    dense_tile = wide // steps
    many = len(pieces)
    rows = many * tokens
    total = -(-(units + share) // LANES) * LANES

    def kernel(place_ref, *refs):
        own, far = refs[:many], refs[many : 2 * many]
        gate_ref, up_ref, gate_in_ref, up_in_ref, dense_ref = refs[2 * many : 2 * many + 5]
        out_ref, x_ref, weight_ref, scale_ref, sums_ref = refs[2 * many + 5 :]
        step = pl.program_id(0)

        @pl.when(step == 0)
        def _():
            lane = lax.broadcasted_iota(jnp.int32, (tokens, LANES), 1)
            expert = place_ref[0] * owned + place_ref[1]
            for i in range(many):
                here = slice(i * tokens, (i + 1) * tokens)
                for side, ref in enumerate((own[i], far[i])):
                    x_ref[here, side * width : (side + 1) * width] = ref[:, :width]
                    x_ref[here, (2 + side) * width : (3 + side) * width] = ref[:, width : 2 * width]
                table = own[i][:, 2 * width :].astype(jnp.float32)
                hit = (lane == expert) | (lane == expert + experts_all)
                weight_ref[here, :] = jnp.sum(jnp.where(hit, table, 0.0), axis=1, keepdims=True)
                table = table + far[i][:, 2 * width :].astype(jnp.float32)
                hit = (lane == 2 * experts_all) | (lane == 2 * experts_all + 1)
                square = jnp.sum(jnp.where(hit, table, 0.0), axis=1, keepdims=True)
                scale_ref[here, :] = 1.0 / jnp.sqrt(square / (2 * width) + 1e-06)

        both = dot(x_ref[:, 2 * width :], dense_ref[...])
        sums_ref[:, pl.ds(pl.multiple_of(step * dense_tile, dense_tile), dense_tile)] = both
        gate_sum = dot(x_ref[:, :width], gate_ref[0]) + dot(x_ref[:, width : 2 * width], gate_in_ref[...])
        up_sum = dot(x_ref[:, :width], up_ref[0]) + dot(x_ref[:, width : 2 * width], up_in_ref[...])
        act = jax.nn.silu(gate_sum) * up_sum * weight_ref[...]
        out_ref[:, pl.ds(pl.multiple_of(step * tile, tile), tile)] = act.astype(jnp.bfloat16)

        @pl.when(step == steps - 1)
        def _():
            scale = scale_ref[...]
            act = jax.nn.silu(sums_ref[:, :main] * scale) * (sums_ref[:, main : 2 * main] * scale)
            out_ref[:, units : units + main] = act.astype(jnp.bfloat16)
            mixed = sums_ref[:, 2 * main :] * scale
            tail = jax.nn.silu(mixed[:, :rest]) * mixed[:, rest:]
            spare = jnp.zeros((rows, total - units - share), jnp.float32)
            out_ref[:, units + main :] = jnp.concatenate([tail, spare], axis=1).astype(jnp.bfloat16)

    def whole(a):
        return pl.BlockSpec(a.shape, lambda j, s: (0, 0))

    own_weight = pl.BlockSpec((1, width, tile), lambda j, s: (s[1], 0, j))
    far_weight = pl.BlockSpec((width, tile), lambda j, s: (0, j))
    return run(
        kernel,
        (place, *pieces, *others, gate, up, gate_in, up_in, dense_rows),
        16 + 4 * (many > 2),
        grid_spec=pltpu.PrefetchScalarGridSpec(
            num_scalar_prefetch=1,
            grid=(steps,),
            in_specs=[whole(p) for p in (*pieces, *others)]
            + [own_weight, own_weight, far_weight, far_weight]
            + [pl.BlockSpec((2 * width, dense_tile), lambda j, s: (0, j))],
            out_specs=pl.BlockSpec((rows, total), lambda j, s: (0, 0)),
            scratch_shapes=[
                pltpu.VMEM((rows, 4 * width), jnp.bfloat16),
                pltpu.VMEM((rows, 1), jnp.float32),
                pltpu.VMEM((rows, 1), jnp.float32),
                pltpu.VMEM((rows, wide), jnp.float32),
            ],
        ),
        out_shape=jax.ShapeDtypeStruct((rows, total), jnp.bfloat16),
        cost_estimate=pl.CostEstimate(
            flops=4 * rows * width * (2 * units + share * 2),
            bytes_accessed=8 * width * units + 2 * rows * 4 * width,
            transcendentals=rows * (units + share),
        ),
    )


def products(place, act, act_in, down, dense_here, dense_in):
    rows = act.shape[0]
    units, width = down.shape[1], down.shape[2]
    share = dense_here.shape[0]
    tile = 512

    def kernel(place_ref, act_ref, in_ref, down_ref, down_far_ref, here_ref, far_ref, keep_ref, send_ref):
        total = dot(act_ref[:, :units], down_ref[0]) + dot(in_ref[:, :units], down_far_ref[0])
        total = total + dot(act_ref[:, units : units + share], here_ref[...])
        total = total + dot(in_ref[:, units : units + share], far_ref[...])
        keep_ref[...] = total[: rows // 2]
        send_ref[...] = total[rows // 2 :].astype(jnp.bfloat16)

    whole = pl.BlockSpec(act.shape, lambda j, s: (0, 0))
    dense = pl.BlockSpec((share, tile), lambda j, s: (0, j))
    piece = pl.BlockSpec((rows // 2, tile), lambda j, s: (0, j))
    return run(
        kernel,
        (place, act, act_in, down, down, dense_here, dense_in),
        14,
        grid_spec=pltpu.PrefetchScalarGridSpec(
            num_scalar_prefetch=1,
            grid=(width // tile,),
            in_specs=[
                whole,
                whole,
                pl.BlockSpec((1, units, tile), lambda j, s: (s[1], 0, j)),
                pl.BlockSpec((1, units, tile), lambda j, s: (1 - s[1], 0, j)),
                dense,
                dense,
            ],
            out_specs=[piece, piece],
        ),
        out_shape=[
            jax.ShapeDtypeStruct((rows // 2, width), jnp.float32),
            jax.ShapeDtypeStruct((rows // 2, width), jnp.bfloat16),
        ],
        cost_estimate=pl.CostEstimate(
            flops=4 * rows * width * (units + share),
            bytes_accessed=4 * width * (units + share) + 4 * rows * width,
            transcendentals=0,
        ),
    )


def local_tiled(
    current,
    previous,
    expert_ids,
    gate_values,
    norm_gain,
    expert_gate,
    expert_up,
    expert_down,
    dense_gate,
    dense_up,
    dense_down,
):
    _, width = previous.shape
    owned = expert_gate.shape[0]
    count = lax.axis_size("expert")
    experts_all = owned * count
    h = lax.axis_index("hidden")
    place = jnp.stack([lax.axis_index("expert"), h, lax.axis_index("groups")]).astype(jnp.int32)

    packed = pack_weights(place, norm_gain.reshape(-1, LANES), dense_gate, dense_up, dense_down, count)
    mine = [packed[0]] + [exchange(packed[j], "expert", j) for j in range(1, count)]
    other = [exchange(mine[j], "groups", 1) for j in range(count)]
    dense_rows, dense_here, dense_there = assemble(place, mine, other, count, width)
    dense_in = exchange(dense_there, "hidden", 1)

    piece = prepare(previous, current, expert_ids, gate_values, experts_all)
    far, near, sides = {}, {}, {}
    for j in range(0, count, 2):
        far[j] = exchange(piece, "expert", j) if j else piece
        near[j] = exchange(far[j], "expert", 1)
        sides[j] = [exchange(far[j], "hidden", 1), exchange(near[j], "hidden", 1)]

    gate_in = exchange(lax.dynamic_index_in_dim(expert_gate, 1 - h, 0, keepdims=False), "hidden", 1)
    up_in = exchange(lax.dynamic_index_in_dim(expert_up, 1 - h, 0, keepdims=False), "hidden", 1)

    result = None
    for j in range(0, count, 2):
        act = activations(
            place, [far[j], near[j]], sides[j], expert_gate, expert_up, gate_in, up_in, dense_rows, experts_all
        )
        act_in = exchange(act, "hidden", 1)
        keep, send = products(place, act, act_in, expert_down, dense_here, dense_in)
        line = keep + exchange(send, "expert", 1).astype(jnp.float32)
        if j:
            line = exchange(line.astype(jnp.bfloat16), "expert", j).astype(jnp.float32)
        result = line if result is None else result + line
    return result.astype(jnp.bfloat16)


def is_tiled(mesh_shape, current, expert_gate, dense_gate, dense_down):
    count = mesh_shape["expert"]
    share = dense_gate.shape[1] // count
    return (
        mesh_shape["hidden"] == mesh_shape["groups"] == expert_gate.shape[0] == 2
        and count == 8
        and share % LANES * 2 == LANES
        and dense_gate.shape[0] == dense_down.shape[1] == 2 * LANES
        and expert_gate.shape[2] % 256 == 0
        and 2 * share % (expert_gate.shape[2] // 256 * LANES) == 0
        and current.shape[1] % 512 == 0
        and 2 * expert_gate.shape[0] * count + 2 <= LANES
    )


def local(*args):
    sizes = {n: lax.axis_size(n) for n in ("expert", "hidden", "groups")}
    if not is_tiled(sizes, args[0], args[5], args[8], args[10]):
        return local_general(*args)
    return local_tiled(*args)


def solution(mesh):
    placed = (
        P(("groups", "expert"), "hidden"),
        P(("groups", "expert"), "hidden"),
        P(("groups", "expert"), None),
        P(("groups", "expert"), None),
        P(),
        P("expert", "hidden", None),
        P("expert", "hidden", None),
        P("expert", None, "hidden"),
        P("expert", "hidden"),
        P("expert", "hidden"),
        P("hidden", "expert"),
    )
    return jax.shard_map(
        local,
        mesh=mesh,
        in_specs=placed,
        out_specs=P(("groups", "expert"), "hidden"),
        check_vma=False,
    )
```

```python
import jax
import jax.numpy as jnp
from jax import lax
from jax.experimental import pallas as pl
from jax.experimental.pallas import tpu as pltpu
from jax.sharding import PartitionSpec as P

TOP_K = 8
LANES = 128


def slot_places(expert_ids, experts_all, owned, owners, capacity):
    flat_ids = expert_ids.reshape(-1)
    one_hot = (flat_ids[:, None] == jnp.arange(experts_all, dtype=jnp.int32)[None, :]).astype(
        jnp.int32
    )
    before = jnp.cumsum(one_hot, axis=0) - one_hot
    position = jnp.sum(before * one_hot, axis=1)
    return flat_ids % owned * (owners * capacity) + flat_ids // owned * capacity + position


def routed_branch(previous, expert_ids, gate_values, expert_gate, expert_up, expert_down):
    tokens_here, slice_width = previous.shape
    owned = expert_gate.shape[0]
    owners = lax.axis_size("expert")
    experts_all = owned * owners
    capacity = min(tokens_here, tokens_here * TOP_K * 9 // (8 * experts_all))
    places = slot_places(expert_ids, experts_all, owned, owners, capacity)
    token_of = jnp.arange(tokens_here * TOP_K, dtype=jnp.int32) // TOP_K
    table = jnp.full((experts_all * capacity,), tokens_here, jnp.int32).at[places].set(token_of)
    routed = previous.astype(jnp.bfloat16)
    routed_pad = jnp.concatenate([routed, jnp.zeros((1, slice_width), jnp.bfloat16)], axis=0)
    outgoing = routed_pad[table].reshape(owned, owners, capacity, slice_width)
    arrived = lax.all_to_all(outgoing, "expert", split_axis=1, concat_axis=1, tiled=True)
    arrived = arrived.reshape(owned, owners * capacity, slice_width)
    gate_part = jnp.einsum("erd,edf->erf", arrived, expert_gate, preferred_element_type=jnp.float32)
    up_part = jnp.einsum("erd,edf->erf", arrived, expert_up, preferred_element_type=jnp.float32)
    gate_sum, up_sum = (
        lax.psum(gate_part.astype(jnp.bfloat16), "hidden").astype(jnp.float32),
        lax.psum(up_part.astype(jnp.bfloat16), "hidden").astype(jnp.float32),
    )
    activated = (jax.nn.silu(gate_sum) * up_sum).astype(jnp.bfloat16)
    produced = jnp.einsum(
        "erf,efd->erd", activated, expert_down, preferred_element_type=jnp.float32
    ).astype(jnp.bfloat16)
    produced = produced.reshape(owned, owners, capacity, slice_width)
    returned = lax.all_to_all(produced, "expert", split_axis=1, concat_axis=1, tiled=True)
    returned = returned.reshape(experts_all * capacity, slice_width)
    picked = returned[places].reshape(tokens_here, TOP_K, slice_width).astype(jnp.float32)
    return jnp.einsum("tk,tkd->td", gate_values, picked)


def dense_branch(current, norm_gain, dense_gate, dense_up, dense_down):
    whole = lax.all_gather(current, "hidden", axis=1, tiled=True)
    wide = whole.astype(jnp.float32)
    mean_square = jnp.mean(wide * wide, axis=1, keepdims=True)
    normed = (wide * norm_gain[None, :] / jnp.sqrt(mean_square + 1e-06)).astype(jnp.bfloat16)
    full_gate, full_up = (
        lax.all_gather(dense_gate, "expert", axis=0, tiled=True),
        lax.all_gather(dense_up, "expert", axis=0, tiled=True),
    )
    gate_dense = jnp.dot(normed, full_gate, preferred_element_type=jnp.float32)
    up_dense = jnp.dot(normed, full_up, preferred_element_type=jnp.float32)
    dense_act = (jax.nn.silu(gate_dense) * up_dense).astype(jnp.bfloat16)
    terms = jnp.dot(
        dense_act,
        lax.all_gather(dense_down, "expert", axis=1, tiled=True),
        preferred_element_type=jnp.float32,
    )
    return lax.psum_scatter(
        terms.astype(jnp.bfloat16), "hidden", scatter_dimension=1, tiled=True
    ).astype(jnp.float32)


def local_general(
    current,
    previous,
    expert_ids,
    gate_values,
    norm_gain,
    expert_gate,
    expert_up,
    expert_down,
    dense_gate,
    dense_up,
    dense_down,
):
    routed_sum = routed_branch(
        previous, expert_ids, gate_values, expert_gate, expert_up, expert_down
    )
    dense_sum = dense_branch(current, norm_gain, dense_gate, dense_up, dense_down)
    return (dense_sum + routed_sum).astype(jnp.bfloat16)


def dot(a, b):
    return jnp.dot(a, b, preferred_element_type=jnp.float32)


def exchange(value, axis, flip):
    return lax.ppermute(value, axis, [(i, i ^ flip) for i in range(lax.axis_size(axis))])


def is_inner(e):
    return ((e >> 1) ^ (e >> 2)) & 1 == 1


def run(kernel, operands, mebibytes, **options):
    return pl.pallas_call(
        kernel, compiler_params=pltpu.CompilerParams(vmem_limit_bytes=mebibytes << 20) if mebibytes else None, **options
    )(*operands)


SMEM = pl.BlockSpec(memory_space=pltpu.SMEM)
VMEM = pl.BlockSpec(memory_space=pltpu.VMEM)


def prepare(previous, current, expert_ids, gate_values, experts_all):
    tokens, width = previous.shape

    def kernel(prev_ref, cur_ref, ids_ref, gates_ref, out_ref):
        out_ref[:, :width] = prev_ref[...].astype(jnp.bfloat16)
        cur = cur_ref[...]
        out_ref[:, width : 2 * width] = cur
        wide = cur.astype(jnp.float32)
        square = jnp.sum(wide * wide, axis=1, keepdims=True)
        row = lax.broadcasted_iota(jnp.int32, (LANES, tokens), 0)
        expert = jnp.where(row < experts_all, row, row - experts_all)
        values = jnp.zeros((LANES, tokens), jnp.float32)
        for k in range(TOP_K):
            hit = expert == ids_ref[k : k + 1, :]
            values = values + jnp.where(hit, gates_ref[k : k + 1, :], 0.0)
        lane = lax.broadcasted_iota(jnp.int32, (tokens, LANES), 1)
        values = jnp.where(lane < 2 * experts_all, values.T, square)
        high = values.astype(jnp.bfloat16).astype(jnp.float32)
        use_low = (lane >= experts_all) & (lane != 2 * experts_all)
        out_ref[:, 2 * width :] = jnp.where(use_low, values - high, high).astype(jnp.bfloat16)

    return run(
        kernel,
        (previous, current, expert_ids.T, gate_values.T),
        0,
        out_shape=jax.ShapeDtypeStruct((tokens, 2 * width + LANES), jnp.bfloat16),
        in_specs=[VMEM] * 4,
        out_specs=VMEM,
    )


def pack_weights(place, gain, dense_gate, dense_up, dense_down, count):
    rows, columns = dense_gate.shape
    share = columns // count
    main, rest = share // LANES * LANES, share % LANES
    half = rows // 2
    low = dense_down.shape[1] // 4

    def kernel(place_ref, gain_ref, gate_ref, up_ref, down_ref, *outs):
        e, g = place_ref[0], place_ref[2]
        line = gain_ref[pl.ds(e * (rows // LANES) + g, 1), :]
        row = lax.broadcasted_iota(jnp.int32, (LANES, LANES), 0)
        lane = lax.broadcasted_iota(jnp.int32, (LANES, LANES), 1)
        scale = jnp.sum(jnp.where(row == lane, line, 0.0), axis=1, keepdims=True)
        rows_here = pl.ds(pl.multiple_of(g * half, LANES), half)
        columns_here = pl.ds(pl.multiple_of(g * 2 * low, LANES), 2 * low)

        def scaled(ref, start):
            block = ref[rows_here, pl.ds(pl.multiple_of(start, LANES), LANES)]
            return block.astype(jnp.float32) * scale

        for index in range(count):
            out_ref = outs[-1].at[index // 2] if index % 2 else outs[index // 2]
            owner = jnp.bitwise_xor(e, index)
            out_ref[:half, :main] = scaled(gate_ref, owner * main).astype(jnp.bfloat16)
            out_ref[:half, main : 2 * main] = scaled(up_ref, owner * main).astype(jnp.bfloat16)
            spot = count * main + owner // 2 * LANES
            tail_gate, tail_up = scaled(gate_ref, spot), scaled(up_ref, spot)
            even = jnp.concatenate([tail_gate[:, :rest], tail_up[:, :rest]], axis=1)
            odd = jnp.concatenate([tail_gate[:, rest:], tail_up[:, rest:]], axis=1)
            out_ref[:half, 2 * main :] = jnp.where(owner % 2 == 0, even, odd).astype(jnp.bfloat16)
            for i in range(main // low):
                start = pl.multiple_of(owner * main + i * low, low)
                out_ref[half:, i * LANES : (i + 1) * LANES] = down_ref[pl.ds(start, low), columns_here]
            start = pl.multiple_of(count * main + owner * rest, rest)
            out_ref[half:, main // low * LANES :] = down_ref[pl.ds(start, low), columns_here]

    block = jax.ShapeDtypeStruct((half + low, 2 * share), jnp.bfloat16)
    stack = jax.ShapeDtypeStruct((count // 2, *block.shape), jnp.bfloat16)
    return run(
        kernel,
        (place, gain, dense_gate, dense_up, dense_down),
        0,
        out_shape=[block] * (count // 2) + [stack],
        in_specs=[SMEM] + [VMEM] * 4,
        out_specs=[VMEM] * (count // 2 + 1),
    )


def blocks_of(stack):
    def kernel(stack_ref, *outs):
        for i, out_ref in enumerate(outs):
            out_ref[...] = stack_ref[i]

    many = stack.shape[0]
    block = jax.ShapeDtypeStruct(stack.shape[1:], stack.dtype)
    return run(kernel, (stack,), 4, out_shape=[block] * many, in_specs=[VMEM], out_specs=[VMEM] * many)


def assemble(place, mine, other, count, width):
    part, wide = mine[0].shape
    share = wide // 2
    half = LANES
    low = part - half
    span = count // 2

    def kernel(place_ref, *refs):
        rows_ref, here_ref, there_ref = refs[-3:]
        e, h, g = place_ref[0], place_ref[1], place_ref[2]
        for blocks, group in ((refs[:count], g), (refs[count : 2 * count], 1 - g)):
            for index, block in enumerate(blocks):
                source = jnp.bitwise_xor(e, index)
                spot = jnp.bitwise_xor(source // span, h) * span + source % span
                start = pl.multiple_of(spot * 2 * half + group * half, half)
                rows_ref[pl.ds(start, half), :] = block[:half]
                lane = pl.ds(pl.multiple_of(source % span * 2 * half + group * half, half), half)
                for side, out_ref in ((h, here_ref), (1 - h, there_ref)):

                    @pl.when(source // span == side)
                    def _():
                        for j in range(share // low):
                            out_ref[j * low : (j + 1) * low, lane] = block[half:, j * half : (j + 1) * half]

    down = jax.ShapeDtypeStruct((share, width), jnp.bfloat16)
    return run(
        kernel,
        (place, *mine, *other),
        10,
        out_shape=[jax.ShapeDtypeStruct((2 * width, wide), jnp.bfloat16), down, down],
        in_specs=[SMEM] + [VMEM] * (2 * count),
        out_specs=[VMEM] * 3,
    )


def activations(place, pieces, others, gate, up, gate_in, up_in, experts_all):
    tokens, width = pieces[0].shape[0], gate.shape[1]
    owned, units = gate.shape[0], gate.shape[2]
    tile = 256
    many = len(pieces)
    rows = many * tokens

    def kernel(place_ref, *refs):
        own, far, tables = refs[:many], refs[many : 2 * many], refs[2 * many : 3 * many]
        gate_ref, up_ref, gate_in_ref, up_in_ref, out_ref, x_ref, weight_ref = refs[3 * many :]

        @pl.when(pl.program_id(0) == 0)
        def _():
            lane = lax.broadcasted_iota(jnp.int32, (tokens, LANES), 1)
            expert = place_ref[0] * owned + place_ref[1]
            hit = (lane == expert) | (lane == expert + experts_all)
            for i in range(many):
                here = slice(i * tokens, (i + 1) * tokens)
                x_ref[here, :width] = own[i][...]
                x_ref[here, width:] = far[i][...]
                table = tables[i][...].astype(jnp.float32)
                weight_ref[here, :] = jnp.sum(jnp.where(hit, table, 0.0), axis=1, keepdims=True)

        gate_sum = dot(x_ref[:, :width], gate_ref[0]) + dot(x_ref[:, width:], gate_in_ref[0])
        up_sum = dot(x_ref[:, :width], up_ref[0]) + dot(x_ref[:, width:], up_in_ref[0])
        act = jax.nn.silu(gate_sum) * up_sum * weight_ref[...]
        out_ref[...] = act.astype(jnp.bfloat16)

    features = pl.BlockSpec((tokens, width), lambda j, s: (0, 0))
    table = pl.BlockSpec((tokens, LANES), lambda j, s: (0, 2 * width // LANES))
    weight = pl.BlockSpec((1, width, tile), lambda j, s: (s[1], 0, j))
    return run(
        kernel,
        (place, *pieces, *others, *pieces, gate, up, gate_in, up_in),
        12,
        grid_spec=pltpu.PrefetchScalarGridSpec(
            num_scalar_prefetch=1,
            grid=(units // tile,),
            in_specs=[features] * (2 * many) + [table] * many + [weight] * 4,
            out_specs=pl.BlockSpec((rows, tile), lambda j, s: (0, j)),
            scratch_shapes=[
                pltpu.VMEM((rows, 2 * width), jnp.bfloat16),
                pltpu.VMEM((rows, 1), jnp.float32),
            ],
        ),
        out_shape=jax.ShapeDtypeStruct((rows, units), jnp.bfloat16),
        cost_estimate=pl.CostEstimate(
            flops=8 * rows * width * units,
            bytes_accessed=8 * width * units + 2 * rows * 2 * width,
            transcendentals=rows * units,
        ),
    )


def dense_activations(pieces, others, dense_rows, experts_all):
    tokens, width = pieces[0].shape[0], dense_rows.shape[0] // 2
    wide = dense_rows.shape[1]
    share = wide // 2
    main = share // LANES * LANES
    rest = share - main
    many = len(pieces)
    pair = 2

    def kernel(*refs):
        own, far = refs[:many], refs[many : 2 * many]
        tables = refs[2 * many : 4 * many]
        dense_ref, out_ref, x_ref = refs[4 * many :]
        lane = lax.broadcasted_iota(jnp.int32, (tokens, LANES), 1)
        hit = (lane == 2 * experts_all) | (lane == 2 * experts_all + 1)
        scales = []
        for i in range(many):
            here = slice(i * tokens, (i + 1) * tokens)
            x_ref[here, :width] = own[i][...]
            x_ref[here, width:] = far[i][...]
            table = tables[i][...].astype(jnp.float32) + tables[many + i][...].astype(jnp.float32)
            square = jnp.sum(jnp.where(hit, table, 0.0), axis=1, keepdims=True)
            scales.append(1.0 / jnp.sqrt(square / (2 * width) + 1e-06))
        for i in range(0, many, pair):
            here = slice(i * tokens, (i + pair) * tokens)
            scale = jnp.concatenate(scales[i : i + pair], axis=0)
            both = dot(x_ref[here, :], dense_ref[...]) * scale
            act = jax.nn.silu(both[:, :main]) * both[:, main : 2 * main]
            tail = jax.nn.silu(both[:, 2 * main : 2 * main + rest]) * both[:, 2 * main + rest :]
            tail = jnp.concatenate([tail, jnp.zeros_like(tail)], axis=1)
            out_ref[here, :main] = act.astype(jnp.bfloat16)
            out_ref[here, main:] = tail.astype(jnp.bfloat16)

    features = pl.BlockSpec((tokens, width), lambda j: (0, 1))
    table = pl.BlockSpec((tokens, LANES), lambda j: (0, 2 * width // LANES))
    rows = many * tokens
    return run(
        kernel,
        (*pieces, *others, *pieces, *others, dense_rows),
        24,
        grid=(1,),
        in_specs=[features] * (2 * many) + [table] * (2 * many) + [pl.BlockSpec(dense_rows.shape, lambda j: (0, 0))],
        out_specs=pl.BlockSpec((rows, main + LANES), lambda j: (0, 0)),
        scratch_shapes=[pltpu.VMEM((rows, 2 * width), jnp.bfloat16)],
        out_shape=jax.ShapeDtypeStruct((rows, main + LANES), jnp.bfloat16),
        cost_estimate=pl.CostEstimate(
            flops=4 * rows * width * wide, bytes_accessed=4 * rows * width, transcendentals=rows * share
        ),
    )


def products(place, chunk, act, act_in, dense, dense_far, down, dense_here, dense_in):
    rows = act.shape[0]
    units, width = down.shape[1], down.shape[2]
    share = dense_here.shape[0]
    tile = 512

    def kernel(place_ref, act_ref, in_ref, own_ref, other_ref, down_ref, down_far_ref, here_ref, far_ref, keep_ref, send_ref):
        total = dot(act_ref[...], down_ref[0]) + dot(in_ref[...], down_far_ref[0])
        total = total + dot(own_ref[:, :share], here_ref[...]) + dot(other_ref[:, :share], far_ref[...])
        keep_ref[...] = total[: rows // 2]
        send_ref[...] = total[rows // 2 :].astype(jnp.bfloat16)

    whole = pl.BlockSpec(act.shape, lambda j, s: (0, 0))
    dense_act = pl.BlockSpec((rows, dense.shape[1]), lambda j, s: (chunk, 0))
    dense_down = pl.BlockSpec((share, tile), lambda j, s: (0, j))
    piece = pl.BlockSpec((rows // 2, tile), lambda j, s: (0, j))
    return run(
        kernel,
        (place, act, act_in, dense, dense_far, down, down, dense_here, dense_in),
        14,
        grid_spec=pltpu.PrefetchScalarGridSpec(
            num_scalar_prefetch=1,
            grid=(width // tile,),
            in_specs=[
                whole,
                whole,
                dense_act,
                dense_act,
                pl.BlockSpec((1, units, tile), lambda j, s: (s[1], 0, j)),
                pl.BlockSpec((1, units, tile), lambda j, s: (1 - s[1], 0, j)),
                dense_down,
                dense_down,
            ],
            out_specs=[piece, piece],
        ),
        out_shape=[
            jax.ShapeDtypeStruct((rows // 2, width), jnp.float32),
            jax.ShapeDtypeStruct((rows // 2, width), jnp.bfloat16),
        ],
        cost_estimate=pl.CostEstimate(
            flops=4 * rows * width * (units + share),
            bytes_accessed=4 * width * (units + share) + 4 * rows * width,
            transcendentals=0,
        ),
    )


def local_tiled(
    current,
    previous,
    expert_ids,
    gate_values,
    norm_gain,
    expert_gate,
    expert_up,
    expert_down,
    dense_gate,
    dense_up,
    dense_down,
):
    _, width = previous.shape
    owned = expert_gate.shape[0]
    count = lax.axis_size("expert")
    experts_all = owned * count
    h = lax.axis_index("hidden")
    place = jnp.stack([lax.axis_index("expert"), h, lax.axis_index("groups")]).astype(jnp.int32)

    *even, odd = pack_weights(place, norm_gain.reshape(-1, LANES), dense_gate, dense_up, dense_down, count)
    odd = blocks_of(exchange(odd, "expert", 1))
    mine = []
    for j in range(count):
        block = odd[j // 2] if j % 2 else even[j // 2]
        mine.append(exchange(block, "expert", j & ~1) if j > 1 else block)
    other = [exchange(m, "groups", 1) for m in mine]
    dense_rows, dense_here, dense_there = assemble(place, mine, other, count, width)
    dense_in = exchange(dense_there, "hidden", 1)

    e = lax.axis_index("expert")
    inner = [i for i in range(count) if is_inner(i)]
    piece = prepare(previous, current, expert_ids, gate_values, experts_all)
    far, near, sides = {0: piece, 2: exchange(piece, "expert", 2)}, {}, {}
    across, outward = {}, {}
    for tag, j in (("1", 0), ("2", 2)):
        across[tag] = lax.ppermute(far[j], "expert", [(i, i ^ 6) for i in inner])
        outward[tag] = lax.ppermute(across[tag], "expert", [(i, i ^ 2) for i in inner])
    for j, held, passed in ((4, "2", "1"), (6, "1", "2")):
        choice = jnp.broadcast_to(is_inner(e), piece.shape)
        far[j] = lax.select(choice, across[held], outward[passed])
    for j in far:
        near[j] = exchange(far[j], "expert", 1)
        sides[j] = [exchange(far[j], "hidden", 1), exchange(near[j], "hidden", 1)]

    gate_in = exchange(expert_gate, "hidden", 1)
    up_in = exchange(expert_up, "hidden", 1)

    acts = {}
    for j in far:
        act = activations(place, [far[j], near[j]], sides[j], expert_gate, expert_up, gate_in, up_in, experts_all)
        acts[j] = act, exchange(act, "hidden", 1)
    dense = {}
    for chunks in ((0, 2, 4), (6,)):
        pieces = [p for j in chunks for p in (far[j], near[j])]
        others = [p for j in chunks for p in sides[j]]
        act = dense_activations(pieces, others, dense_rows, experts_all)
        act_in = exchange(act, "hidden", 1)
        dense.update({j: (i, act, act_in) for i, j in enumerate(chunks)})
    result = None
    for j in far:
        chunk, *dense_acts = dense[j]
        keep, leave = products(place, chunk, *acts[j], *dense_acts, expert_down, dense_here, dense_in)
        line = keep + exchange(leave, "expert", 1).astype(jnp.float32)
        if j:
            line = exchange(line.astype(jnp.bfloat16), "expert", j).astype(jnp.float32)
        result = line if result is None else result + line
    return result.astype(jnp.bfloat16)


def is_tiled(mesh_shape, current, expert_gate, dense_gate, dense_down):
    count = mesh_shape["expert"]
    share = dense_gate.shape[1] // count
    return (
        mesh_shape["hidden"] == mesh_shape["groups"] == expert_gate.shape[0] == 2
        and count == 8
        and share % LANES * 2 == LANES
        and dense_gate.shape[0] == dense_down.shape[1] == 2 * LANES
        and expert_gate.shape[2] % 256 == 0
        and 2 * share % (expert_gate.shape[2] // 256 * LANES) == 0
        and current.shape[1] % 512 == 0
        and 2 * expert_gate.shape[0] * count + 2 <= LANES
    )


def local(*args):
    sizes = {n: lax.axis_size(n) for n in ("expert", "hidden", "groups")}
    if not is_tiled(sizes, args[0], args[5], args[8], args[10]):
        return local_general(*args)
    return local_tiled(*args)


def solution(mesh):
    placed = (
        P(("groups", "expert"), "hidden"),
        P(("groups", "expert"), "hidden"),
        P(("groups", "expert"), None),
        P(("groups", "expert"), None),
        P(),
        P("expert", "hidden", None),
        P("expert", "hidden", None),
        P("expert", None, "hidden"),
        P("expert", "hidden"),
        P("expert", "hidden"),
        P("hidden", "expert"),
    )
    return jax.shard_map(
        local,
        mesh=mesh,
        in_specs=placed,
        out_specs=P(("groups", "expert"), "hidden"),
        check_vma=False,
    )
```
